128 devices in a mesh: seq: 64 (over y_lo, x, z, core), fsdp: 2 (over y_hi).
Axes of the slice: x: 4, y: 4 (y_hi: 2, y_lo: 2; y = y_hi * 2 + y_lo), z: 4, core: 2. Of those that a mesh axis runs over, the one named last changes fastest.
Arguments:
- state_in: bfloat16 [8192, 5280], P('seq'), may hold values from -6 to 6
- query_vectors: bfloat16 [8192, 2688], P('seq', 'fsdp'), may hold values from -6 to 6
- key_vectors: bfloat16 [8192, 2688], P('seq', 'fsdp'), may hold values from -6 to 6
- value_weight: bfloat16 [2, 1344, 5280], P('fsdp', 'seq'), may hold values from -0.078125 to 0.078125
- out_weight: bfloat16 [2, 1344, 5280], P('fsdp', 'seq'), may hold values from -0.3125 to 0.3125
- doc_ids: int32 [64], replicated, may hold values from 0 to 20, never falling along the last dimension, each value on 1 to 5 neighbouring positions
- cotangent: bfloat16 [8192, 5280], P('seq'), may hold values from -6 to 6
Outputs:
- final_state: bfloat16 [8192, 5280], P('seq')
- state_grad: float32 [8192, 5280], P('seq')
The draws below stay inside these ranges and needn't reach their ends.
Inputs may be any that keep to these rules, and one draw needn't show every extreme that they name: `doc_ids`: document ids never fall along the blocks; each document covers 1 to 5 consecutive blocks, and some document covers exactly 5.
All inputs are finite; a program needn't handle non-finite values.
Results may differ from the reference program's by a relative error of at most 0.013.
Values may be sent and summed in bfloat16 or wider, within the bound.
No kernel may reach another device: no remote copies, remote signals or barrier semaphores. Data moves between devices by JAX's collectives and lax.ppermute only.
A program may use at most 256 MiB of HBM per device.

```python
import math
import jax
import jax.numpy as jnp
import numpy as np
from jax import lax

D = 5280
HEADS = 28
HEAD_DIM = 96
BLOCK = 128
DOC_BLOCKS = 5
UNROLL = 2
TOK_DEV = 128
HEAD_WIDTH = 2688
SEQ_LEN = 8192
NUM_BLOCKS = 64
REACH = 4
DOC_COUNT = 21
N_FSDP = 2


def paired_vectors(key):
    base_seed = jax.random.fold_in(key, 1234)
    seed_query, seed_keys = jax.random.split(base_seed, 2)
    array_shape = (SEQ_LEN, HEAD_WIDTH)
    query_part = jnp.clip(jax.random.normal(seed_query, array_shape, jnp.float32), -6.0, 6.0)
    key_part = jnp.clip(jax.random.normal(seed_keys, array_shape, jnp.float32), -6.0, 6.0)
    return (query_part, key_part)


def draw_query_vectors(key, part):
    return paired_vectors(key)[0].astype(jnp.bfloat16)


def draw_key_vectors(key, part):
    return paired_vectors(key)[1].astype(jnp.bfloat16)


def block_levels(own_key, extent, shards, least, top_value):
    loudness, own = 1.0, jax.random.fold_in(own_key, 6)
    for dim, shards_of in shards:
        draws = jnp.exp(jax.random.uniform(jax.random.fold_in(own, dim), (shards_of,), jnp.float32, least / len(shards), top_value / len(shards)))
        loudness = loudness * jnp.repeat(draws, extent[dim] // shards_of).reshape([-1 if axis == dim else 1 for axis in range(len(extent))])
    return loudness


def profile(amount, total, reach, slope):
    portions = [(1 << 20) // math.isqrt(standing ** slope) + 1 for standing in range(2, amount + 1)]
    rest, given = total - reach - (amount - 1), [1] * (amount - 1)
    while rest > 0:
        candidates = [i for i in range(amount - 1) if given[i] < reach]
        whole, left = sum([portions[i] for i in candidates]), rest
        for i in candidates:
            addition = min(reach - given[i], max(1, left * portions[i] // whole), rest)
            given[i] = given[i] + addition
            rest = rest - addition
    return np.array([reach] + given)


def uneven_parts(rng, amount, total, most, slope):
    if amount == 2:
        one = jax.random.randint(rng, (), max(1, total - most), min(most, total - 1) + 1)
        return jnp.stack([one, total - one])
    tallies = jnp.asarray(profile(amount, total, most, slope), jnp.int32)
    pairs = (amount - 1) // 2
    donor, receiver = tallies[1:1 + 2 * pairs:2], tallies[2:2 + 2 * pairs:2]
    room = jnp.minimum(donor - 1, most - receiver)
    shifted = jax.random.randint(jax.random.fold_in(rng, 1), (pairs,), 0, 1 << 20) % (room + 1)
    tallies = tallies.at[1:1 + 2 * pairs:2].set(donor - shifted).at[2:2 + 2 * pairs:2].set(receiver + shifted)
    return tallies[jax.random.permutation(jax.random.fold_in(rng, 2), amount)]


def bell_draw(stream_key, shape, width, reach, cuts=(), kind=jnp.bfloat16):
    values = jax.random.normal(stream_key, shape, jnp.float32) * width
    if len(cuts) > 0:
        values = block_levels(stream_key, shape, cuts, -0.22, 0.18) * values
    return jnp.clip(values, min=-reach, max=reach).astype(kind)


def setup_inputs(seed: int = 0) -> dict:
    streams_of = jax.random.split(jax.random.key(seed), 8)
    state_in = bell_draw(streams_of[0], (SEQ_LEN, D), 1.0, 6.0, ((0, 64),))
    query_vectors = draw_query_vectors(jax.random.fold_in(streams_of[7], 71), 0)
    key_vectors = draw_key_vectors(jax.random.fold_in(streams_of[7], 71), 0)
    value_weight = bell_draw(streams_of[3], (N_FSDP, HEAD_WIDTH // N_FSDP, D), D ** -0.5, 0.078125, ((0, 2), (1, 64)))
    out_weight = bell_draw(streams_of[4], (N_FSDP, HEAD_WIDTH // N_FSDP, D), (HEAD_WIDTH // 8) ** -0.5, 0.3125, ((0, 2), (1, 64)))
    doc_ids = jnp.searchsorted(jnp.cumsum(uneven_parts(streams_of[5], DOC_COUNT, NUM_BLOCKS, DOC_BLOCKS, 0)), jnp.arange(NUM_BLOCKS), side="right").astype(jnp.int32)
    cotangent = bell_draw(streams_of[6], (SEQ_LEN, D), 1.0, 6.0, ((0, 64),))
    return {"state_in": state_in, "query_vectors": query_vectors, "key_vectors": key_vectors, "value_weight": value_weight, "out_weight": out_weight, "doc_ids": doc_ids, "cotangent": cotangent}


epsilon = 1e-06

def normalize(current):
    mean_square = lax.optimization_barrier(jnp.mean(current * current, axis=-1, keepdims=True))
    inverse_rms = lax.rsqrt(mean_square + epsilon)
    return (current * inverse_rms, inverse_rms)

def rounded(array):
    return lax.optimization_barrier(array.astype(jnp.bfloat16)).astype(jnp.float32)

def grouped(left, right_groups):
    group_width = HEAD_WIDTH // N_FSDP
    running = jnp.zeros((left.shape[0], D), jnp.float32)
    for group in range(N_FSDP):
        columns = left[:, group * group_width:(group + 1) * group_width]
        running = running + rounded(jnp.dot(columns, right_groups[group], preferred_element_type=jnp.float32))
    return running

def reference(state_in, query_vectors, key_vectors, value_weight, out_weight, doc_ids, cotangent):
    rows_here = TOK_DEV
    blocks_here = TOK_DEV // BLOCK
    window_rows = (REACH + 1) * rows_here
    pad_rows = REACH * rows_here
    device_count = SEQ_LEN // TOK_DEV
    value_full = value_weight.reshape(HEAD_WIDTH, D)
    out_full = out_weight.reshape(HEAD_WIDTH, D)
    key_padded = jnp.concatenate([jnp.zeros((pad_rows, HEAD_WIDTH), key_vectors.dtype), key_vectors], 0)
    doc_padded = jnp.concatenate([jnp.full((REACH * blocks_here,), -1, jnp.int32), doc_ids.astype(jnp.int32)])
    query_heads = query_vectors.reshape(device_count, rows_here, HEADS, HEAD_DIM)
    slot_rows = jnp.arange(window_rows)
    query_rows = jnp.arange(rows_here) + pad_rows
    score_scale = 1.0 / math.sqrt(HEAD_DIM)
    device_ids = jnp.arange(device_count, dtype=jnp.int32)

    def device_probs(device):
        start = (device * rows_here).astype(jnp.int32)
        window_keys = lax.dynamic_slice_in_dim(key_padded, start, window_rows, 0).reshape(window_rows, HEADS, HEAD_DIM)
        window_docs = lax.dynamic_slice_in_dim(doc_padded, (device * blocks_here).astype(jnp.int32), (REACH + 1) * blocks_here, 0)
        key_docs = jnp.broadcast_to(window_docs[:, None], ((REACH + 1) * blocks_here, BLOCK)).reshape(-1)
        query_docs = key_docs[pad_rows:]
        allowed = (key_docs[None, :] == query_docs[:, None]) & (slot_rows[None, :] <= query_rows[:, None])
        queries_here = query_heads[device]
        scores = jnp.einsum('qhd,khd->hqk', queries_here.astype(jnp.float32), window_keys.astype(jnp.float32)) * score_scale
        masked = jnp.where(allowed[None], scores, -1e+30)
        maxima = lax.optimization_barrier(jnp.max(masked, axis=2, keepdims=True))
        raised = jnp.where(allowed[None], jnp.exp(masked - maxima), 0.0)
        denominator = lax.optimization_barrier(jnp.sum(raised, axis=2, keepdims=True))
        return (raised / denominator).astype(jnp.bfloat16)
    all_probs = lax.map(device_probs, device_ids)

    def attend(values_b):
        padded = jnp.concatenate([jnp.zeros((pad_rows, HEAD_WIDTH), values_b.dtype), values_b], 0)

        def one_device(device):
            window_values = lax.dynamic_slice_in_dim(padded, (device * rows_here).astype(jnp.int32), window_rows, 0)
            window_values = window_values.reshape(window_rows, HEADS, HEAD_DIM)
            result = jnp.einsum('hqk,khd->qhd', all_probs[device].astype(jnp.float32), window_values.astype(jnp.float32))
            return result.reshape(rows_here, HEAD_WIDTH).astype(jnp.bfloat16)
        return lax.map(one_device, device_ids).reshape(SEQ_LEN, HEAD_WIDTH)

    def spread(d_attended):
        d_heads = d_attended.reshape(device_count, rows_here, HEADS, HEAD_DIM)

        def one_device(device):
            slot_terms = jnp.einsum('hqk,qhd->khd', all_probs[device].astype(jnp.float32), d_heads[device].astype(jnp.float32))
            return slot_terms.reshape(REACH + 1, rows_here, HEAD_WIDTH).astype(jnp.bfloat16)
        all_terms = lax.map(one_device, device_ids)
        running = jnp.zeros((device_count, rows_here, HEAD_WIDTH), jnp.float32)
        for distance in range(REACH + 1):
            contrib = all_terms[distance:, REACH - distance].astype(jnp.float32)
            filler = jnp.zeros((distance, rows_here, HEAD_WIDTH), jnp.float32)
            running = running + jnp.concatenate([contrib, filler], 0)
        return running.reshape(SEQ_LEN, HEAD_WIDTH).astype(jnp.bfloat16)
    value_groups = value_weight
    out_groups = out_weight
    current = state_in.astype(jnp.float32)
    records = []
    for unroll_step in range(UNROLL):
        normed, inverse_rms = normalize(current)
        values_b = lax.dot_general(normed.astype(jnp.bfloat16), value_full, (((1,), (1,)), ((), ())), preferred_element_type=jnp.float32).astype(jnp.bfloat16)
        attended = attend(values_b)
        current = current + grouped(attended, out_groups)
        records.append((normed, inverse_rms))
    final_state = current.astype(jnp.bfloat16)
    gradient = cotangent.astype(jnp.float32)
    for normed, inverse_rms in reversed(records):
        grad_b = gradient.astype(jnp.bfloat16)
        d_attended = lax.dot_general(grad_b, out_full, (((1,), (1,)), ((), ())), preferred_element_type=jnp.float32).astype(jnp.bfloat16)
        dvalues = spread(d_attended)
        d_normed = grouped(dvalues, value_groups)
        gradient = gradient + inverse_rms * (d_normed - normed * lax.optimization_barrier(jnp.mean(d_normed * normed, axis=-1, keepdims=True)))
    return (final_state, gradient)
```

```python
import math

import jax
import jax.numpy as jnp
from jax import lax
from jax.experimental import pallas as pl
from jax.experimental.pallas import tpu as pltpu
from jax.sharding import Mesh
from jax.sharding import PartitionSpec as P

HEAD_DIM = 96
BLOCK = 128
UNROLL = 2
REACH = 4
EPS = 1e-06

D = 5280
QF = 1320
T = 256
HQ = 672
HEADS_Q = 7
UNIT = 24
NPAD = 768
CHIPS = 32

bf16 = jnp.bfloat16
f32 = jnp.float32
PARAMS = pltpu.CompilerParams(vmem_limit_bytes=56 * 1024 * 1024)
SWAP = [(0, 1), (1, 0)]


def window(h):
    lo = (HEAD_DIM * h) // 128 * 128
    hi = min(-(-(HEAD_DIM * (h + 1)) // 128) * 128, HQ)
    return lo, hi


def head_mask(h, lo, hi):
    lane = lax.broadcasted_iota(jnp.int32, (1, hi - lo), 1) + lo
    return (lane >= HEAD_DIM * h) & (lane < HEAD_DIM * (h + 1))


def dot_t(a, b):
    return lax.dot_general(a, b, (((1,), (1,)), ((), ())), preferred_element_type=f32)


def dot(a, b):
    return jnp.dot(a, b, preferred_element_type=f32)


def project_body(sel, x_ref, g_ref, ss_ref, o_ref, *, stats):
    w = g_ref[...].reshape(NPAD, QF)
    out = dot_t(x_ref[...], w)
    if stats:
        ss = ss_ref[...]
        hi = ss.astype(bf16).astype(f32)
        lo = ss - hi
        lane = lax.broadcasted_iota(jnp.int32, (1, NPAD), 1)
        spot = UNIT * sel[2] + 21
        out = out + jnp.where(lane == spot, hi, 0.0) + jnp.where(lane == spot + 1, lo, 0.0)
    o_ref[0] = out.astype(bf16)


def project(x, g, ss, sel, stats):
    import functools

    return pl.pallas_call(
        functools.partial(project_body, stats=stats),
        out_shape=jax.ShapeDtypeStruct((2, T, NPAD), bf16),
        grid_spec=pltpu.PrefetchScalarGridSpec(
            num_scalar_prefetch=1,
            grid=(2,),
            in_specs=[
                pl.BlockSpec((T, QF), lambda i, s: (0, 0)),
                pl.BlockSpec((16, 1, 48, QF), lambda i, s: (0, s[i], 0, 0)),
                pl.BlockSpec((T, 1), lambda i, s: (0, 0)),
            ],
            out_specs=pl.BlockSpec((1, T, NPAD), lambda i, s: (i, 0, 0)),
        ),
        compiler_params=PARAMS,
        name="project",
    )(sel, x, g, ss)


def settle_body(k_ref, c_ref, f_ref, sel_ref, v_ref, inv_ref):
    v = k_ref[0].astype(f32) + c_ref[0].astype(f32) + f_ref[...].astype(f32)
    lane = lax.broadcasted_iota(jnp.int32, (1, 128), 1)
    spot = lane % UNIT
    mark = ((spot == 21) | (spot == 22)) & (lane < 4 * UNIT)
    ss = jnp.sum(jnp.where(mark, v[:, :128], 0.0), axis=1, keepdims=True)
    inv = lax.rsqrt(ss * (1.0 / D) + EPS)
    v_ref[...] = dot((v * inv).astype(bf16), sel_ref[...]).astype(bf16)
    inv_ref[...] = inv


def settle(kept, from_core, from_f, onehot):
    first = pl.BlockSpec((1, T, NPAD), lambda i: (0, 0, 0))
    return pl.pallas_call(
        settle_body,
        out_shape=(jax.ShapeDtypeStruct((T, HQ), bf16), jax.ShapeDtypeStruct((T, 1), f32)),
        grid=(1,),
        out_specs=(
            pl.BlockSpec((T, HQ), lambda i: (0, 0)),
            pl.BlockSpec((T, 1), lambda i: (0, 0)),
        ),
        in_specs=[
            first,
            first,
            pl.BlockSpec((T, NPAD), lambda i: (0, 0)),
            pl.BlockSpec((NPAD, HQ), lambda i: (0, 0)),
        ],
        compiler_params=PARAMS,
        name="settle",
    )(kept, from_core, from_f, onehot)


def softmax_body(q_ref, k2_ref, k1_ref, k0_ref, qd_ref, kd_ref, p_ref, pt_ref):
    row = lax.broadcasted_iota(jnp.int32, (T, 3 * T), 0)
    col = lax.broadcasted_iota(jnp.int32, (T, 3 * T), 1)
    ok = (qd_ref[...] == kd_ref[...]) & (col <= row + 2 * T)
    scale = 1.0 / math.sqrt(HEAD_DIM)
    for h in range(HEADS_Q):
        lo, hi = window(h)
        q = jnp.where(head_mask(h, lo, hi), q_ref[:, lo:hi].astype(f32), 0.0).astype(bf16)
        s = jnp.concatenate(
            [dot_t(q, k2_ref[:, lo:hi]), dot_t(q, k1_ref[:, lo:hi]), dot_t(q, k0_ref[:, lo:hi])],
            axis=1,
        )
        s = jnp.where(ok, s * scale, -1e30)
        top = jnp.max(s, axis=1, keepdims=True)
        e = jnp.where(ok, jnp.exp(s - top), 0.0)
        p = e / jnp.sum(e, axis=1, keepdims=True)
        p_ref[h] = p.astype(bf16)
        pt_ref[h] = p.T.astype(bf16)


def softmax(q, k2, k1, k0, qdoc, kdoc):
    return pl.pallas_call(
        softmax_body,
        out_shape=(
            jax.ShapeDtypeStruct((HEADS_Q, T, 3 * T), bf16),
            jax.ShapeDtypeStruct((HEADS_Q, 3 * T, T), bf16),
        ),
        compiler_params=PARAMS,
        name="softmax",
    )(q, k2, k1, k0, qdoc, kdoc)


def attend_body(p_ref, v2_ref, v1_ref, v0_ref, sel_ref, o_ref, acc_ref):
    acc_ref[...] = jnp.zeros_like(acc_ref)
    for h in range(HEADS_Q):
        lo, hi = window(h)
        out = (
            dot(p_ref[h, :, :T], v2_ref[:, lo:hi])
            + dot(p_ref[h, :, T : 2 * T], v1_ref[:, lo:hi])
            + dot(p_ref[h, :, 2 * T :], v0_ref[:, lo:hi])
        )
        acc_ref[:, lo:hi] += jnp.where(head_mask(h, lo, hi), out, 0.0)
    o_ref[...] = dot_t(acc_ref[...].astype(bf16), sel_ref[...]).astype(bf16)


def attend(p, v2, v1, v0, onehot):
    return pl.pallas_call(
        attend_body,
        out_shape=jax.ShapeDtypeStruct((T, NPAD), bf16),
        scratch_shapes=[pltpu.VMEM((T, HQ), f32)],
        compiler_params=PARAMS,
        name="attend",
    )(p, v2, v1, v0, onehot)


def spread_body(k_ref, c_ref, f_ref, sel_ref, pt_ref, o2_ref, o1_ref, o0_ref, acc_ref):
    v = k_ref[0].astype(f32) + c_ref[0].astype(f32) + f_ref[...].astype(f32)
    da = dot(v.astype(bf16), sel_ref[...]).astype(bf16)
    acc_ref[...] = jnp.zeros_like(acc_ref)
    for h in range(HEADS_Q):
        lo, hi = window(h)
        out = dot(pt_ref[h], da[:, lo:hi])
        acc_ref[:, lo:hi] += jnp.where(head_mask(h, lo, hi), out, 0.0)
    o2_ref[...] = acc_ref[:T].astype(bf16)
    o1_ref[...] = acc_ref[T : 2 * T].astype(bf16)
    o0_ref[...] = acc_ref[2 * T :].astype(bf16)


def spread(kept, from_core, from_f, onehot, pt):
    first = pl.BlockSpec((1, T, NPAD), lambda i: (0, 0, 0))
    one = jax.ShapeDtypeStruct((T, HQ), bf16)
    return pl.pallas_call(
        spread_body,
        out_shape=(one, one, one),
        grid=(1,),
        out_specs=(pl.BlockSpec((T, HQ), lambda i: (0, 0)),) * 3,
        in_specs=[
            first,
            first,
            pl.BlockSpec((T, NPAD), lambda i: (0, 0)),
            pl.BlockSpec((NPAD, HQ), lambda i: (0, 0)),
            pl.BlockSpec((HEADS_Q, 3 * T, T), lambda i: (0, 0, 0)),
        ],
        scratch_shapes=[pltpu.VMEM((3 * T, HQ), f32)],
        compiler_params=PARAMS,
        name="spread",
    )(kept, from_core, from_f, onehot, pt)


def gather_grad_body(o_ref, r1_ref, r2_ref, v_ref, sel_ref, out_ref):
    dv = o_ref[...].astype(f32) + r1_ref[...].astype(f32) + r2_ref[...].astype(f32)
    dv = dv.astype(bf16)
    m = jnp.sum(dv.astype(f32) * v_ref[...].astype(f32), axis=1, keepdims=True)
    hi = m.astype(bf16).astype(f32)
    lo = m - hi
    lane = lax.broadcasted_iota(jnp.int32, (1, NPAD), 1)
    out = dot_t(dv, sel_ref[...])
    out = out + jnp.where(lane == 21, hi, 0.0) + jnp.where(lane == 22, lo, 0.0)
    out_ref[...] = out.astype(bf16)


def gather_grad(own, r1, r2, values, onehot):
    return pl.pallas_call(
        gather_grad_body,
        out_shape=jax.ShapeDtypeStruct((T, NPAD), bf16),
        compiler_params=PARAMS,
        name="gather_grad",
    )(own, r1, r2, values, onehot)


def half_body(sel, a_ref, b_ref, g_ref, base_ref, o_ref):
    i = pl.program_id(0)
    w = g_ref[...].reshape(NPAD, QF)

    @pl.when(i == 0)
    def _():
        o_ref[...] = base_ref[...] + dot(a_ref[...], w)

    @pl.when(i == 1)
    def _():
        o_ref[...] += dot(b_ref[...], w)


def half(a, b, g, base, sel):
    full = pl.BlockSpec((T, NPAD), lambda i, s: (0, 0))
    wide = pl.BlockSpec((T, QF), lambda i, s: (0, 0))
    return pl.pallas_call(
        half_body,
        out_shape=jax.ShapeDtypeStruct((T, QF), f32),
        grid_spec=pltpu.PrefetchScalarGridSpec(
            num_scalar_prefetch=1,
            grid=(2,),
            in_specs=[
                full,
                full,
                pl.BlockSpec((16, 1, 48, QF), lambda i, s: (0, s[i], 0, 0)),
                wide,
            ],
            out_specs=wide,
        ),
        compiler_params=PARAMS,
        name="half",
    )(sel, a, b, g, base)


def update_body(sel, a_ref, b_ref, g_ref, part_ref, o_ref, x_ref, ss_ref):
    i = pl.program_id(0)
    w = g_ref[...].reshape(NPAD, QF)

    @pl.when(i == 0)
    def _():
        o_ref[...] = part_ref[...] + dot(a_ref[...], w)

    @pl.when(i == 1)
    def _():
        new = o_ref[...] + dot(b_ref[...], w)
        o_ref[...] = new
        x_ref[...] = new.astype(bf16)
        ss_ref[...] = jnp.sum(new * new, axis=1, keepdims=True)


def update(a, b, g, part, sel):
    full = pl.BlockSpec((T, NPAD), lambda i, s: (0, 0))
    wide = pl.BlockSpec((T, QF), lambda i, s: (0, 0))
    return pl.pallas_call(
        update_body,
        out_shape=(
            jax.ShapeDtypeStruct((T, QF), f32),
            jax.ShapeDtypeStruct((T, QF), bf16),
            jax.ShapeDtypeStruct((T, 1), f32),
        ),
        grid_spec=pltpu.PrefetchScalarGridSpec(
            num_scalar_prefetch=1,
            grid=(2,),
            in_specs=[
                full,
                full,
                pl.BlockSpec((16, 1, 48, QF), lambda i, s: (0, s[i], 0, 0)),
                wide,
            ],
            out_specs=(wide, wide, pl.BlockSpec((T, 1), lambda i, s: (0, 0))),
        ),
        compiler_params=PARAMS,
        name="update",
    )(sel, a, b, g, part)


def backstep_body(sel, a_ref, b_ref, c_ref, d_ref, g_ref, part_ref, grad_ref, cur_ref, inv_ref, o_ref, x_ref, acc_ref):
    i = pl.program_id(0)
    w = g_ref[...].reshape(NPAD, QF)

    @pl.when(i == 0)
    def _():
        acc_ref[...] = part_ref[...] + dot(a_ref[...], w)

    @pl.when(i == 1)
    def _():
        d_normed = acc_ref[...] + dot(b_ref[...], w)
        lane = lax.broadcasted_iota(jnp.int32, (1, 128), 1)
        mark = (lane == 21) | (lane == 22)
        m = jnp.zeros((T, 1), f32)
        for r in (a_ref, b_ref, c_ref, d_ref):
            m = m + jnp.sum(jnp.where(mark, r[:, :128].astype(f32), 0.0), axis=1, keepdims=True)
        inv = inv_ref[...]
        new = grad_ref[...] + inv * (d_normed - cur_ref[...] * (inv * m * (1.0 / D)))
        o_ref[...] = new
        x_ref[...] = new.astype(bf16)


def backstep(a, b, c, d, g, part, grad, current, inv, sel):
    full = pl.BlockSpec((T, NPAD), lambda i, s: (0, 0))
    wide = pl.BlockSpec((T, QF), lambda i, s: (0, 0))
    return pl.pallas_call(
        backstep_body,
        out_shape=(jax.ShapeDtypeStruct((T, QF), f32), jax.ShapeDtypeStruct((T, QF), bf16)),
        grid_spec=pltpu.PrefetchScalarGridSpec(
            num_scalar_prefetch=1,
            grid=(2,),
            in_specs=[
                full,
                full,
                full,
                full,
                pl.BlockSpec((16, 1, 48, QF), lambda i, s: (0, s[i], 0, 0)),
                wide,
                wide,
                wide,
                pl.BlockSpec((T, 1), lambda i, s: (0, 0)),
            ],
            out_specs=(wide, wide),
            scratch_shapes=[pltpu.VMEM((T, QF), f32)],
        ),
        compiler_params=PARAMS,
        name="backstep",
    )(sel, a, b, c, d, g, part, grad, current, inv)


def assemble_body(sel, a_ref, b_ref, c_ref, d_ref, o_ref):
    for mine in range(4):

        @pl.when(sel[0] == mine)
        def _(mine=mine):
            f, c = mine // 2, mine % 2
            spots = (2 * f + c, 2 * f + 1 - c, 2 * (1 - f) + c, 2 * (1 - f) + 1 - c)
            for q, r in zip(spots, (a_ref, b_ref, c_ref, d_ref)):
                o_ref[:, q * QF : (q + 1) * QF] = r[...].astype(o_ref.dtype)


def assemble(a, b, c, d, sel, dtype):
    part = pl.BlockSpec((BLOCK, QF), lambda i, s: (0, 0))
    return pl.pallas_call(
        assemble_body,
        out_shape=jax.ShapeDtypeStruct((BLOCK, D), dtype),
        grid_spec=pltpu.PrefetchScalarGridSpec(
            num_scalar_prefetch=1,
            grid=(1,),
            in_specs=[part] * 4,
            out_specs=pl.BlockSpec((BLOCK, D), lambda i, s: (0, 0)),
        ),
        compiler_params=PARAMS,
        name="assemble",
    )(sel, a, b, c, d)


def swap_c(x):
    return lax.ppermute(x, "c", SWAP)


def swap_f(x):
    return lax.ppermute(x, "f", SWAP)


def along(x, steps):
    pairs = [(i, i + steps) for i in range(CHIPS) if 0 <= i + steps < CHIPS]
    return lax.ppermute(x, ("yl", "x", "z"), pairs)


def weight_quarter(w):
    rows = jnp.pad(w[0], ((0, UNIT - w.shape[1]), (0, 0)))
    quarters = rows.reshape(UNIT, 2, 2, QF).transpose(1, 2, 0, 3)
    sent = jnp.broadcast_to(quarters[:, None], (2, 2, 2, UNIT, QF)).reshape(8, UNIT, QF)
    got = lax.all_to_all(sent, ("f", "yl", "c"), 0, 0, tiled=True)
    return got.reshape(4, 2 * UNIT, QF)


def token_quarter(x, f):
    part = lax.dynamic_slice_in_dim(x, f * (2 * QF), 2 * QF, 1)
    part = part.reshape(BLOCK, 2, QF).transpose(1, 0, 2)
    return lax.all_to_all(part, "c", 0, 0, tiled=True).reshape(T, QF)


def head_quarter(x):
    part = x.reshape(BLOCK, 2, HQ).transpose(1, 0, 2)
    return lax.all_to_all(part, "c", 0, 0, tiled=True).reshape(T, HQ)


def own_tokens(x, c):
    mine = lax.dynamic_slice_in_dim(x, c * BLOCK, BLOCK, 0)
    theirs = lax.dynamic_slice_in_dim(x, (1 - c) * BLOCK, BLOCK, 0)
    other = swap_c(theirs)
    far = swap_f(mine)
    far_other = swap_f(other)
    return mine, other, far, far_other


def reduced(x, g, ss, away, here, stats):
    sent = project(x, g, ss, away, stats)
    from_core = swap_c(sent)
    kept = project(x, g, ss, here, stats)
    from_f = swap_f(kept[1] + from_core[1])
    return kept, from_core, from_f


def local(state_in, query_vectors, key_vectors, value_weight, out_weight, doc_ids, cotangent):
    c = lax.axis_index("c")
    f = lax.axis_index("f")
    chip = (lax.axis_index("yl") * 4 + lax.axis_index("x")) * 4 + lax.axis_index("z")
    me = 2 * f + c
    near_f = 2 * f + (1 - c)
    far_c = 2 * (1 - f) + c
    far_d = 2 * (1 - f) + (1 - c)
    here = jnp.stack([me, far_c, me]).astype(jnp.int32)
    away = jnp.stack([near_f, far_d, me]).astype(jnp.int32)
    first = jnp.stack([me, near_f]).astype(jnp.int32)
    second = jnp.stack([far_c, far_d]).astype(jnp.int32)

    value_part = weight_quarter(value_weight)
    values_w = lax.all_gather(value_part, ("x", "z"), axis=0)
    out_part = weight_quarter(out_weight)
    out_w = lax.all_gather(out_part, ("x", "z"), axis=0)

    k_pad = jnp.arange(NPAD)[:, None]
    k_nat = jnp.arange(HQ)[None, :]
    onehot = ((k_pad // UNIT * 21 + k_pad % UNIT == k_nat) & (k_pad % UNIT < 21)).astype(bf16)

    docs = jnp.concatenate([jnp.full((REACH,), -1, jnp.int32), doc_ids])
    docs = lax.dynamic_slice_in_dim(docs, 2 * chip, REACH + 2, 0)
    kdoc = jnp.broadcast_to(docs[:, None], (REACH + 2, BLOCK)).reshape(1, 3 * T)
    qdoc = jnp.broadcast_to(docs[REACH:, None], (2, BLOCK)).reshape(T, 1)
    q = head_quarter(query_vectors)
    k = head_quarter(key_vectors)
    p, pt = softmax(q, along(k, 2), along(k, 1), k, qdoc, kdoc)

    x = token_quarter(state_in, f)
    gb = token_quarter(cotangent, f)
    current = x.astype(f32)
    ss = jnp.sum(current * current, axis=1, keepdims=True)
    records = []
    for _ in range(UNROLL):
        kept, from_core, from_f = reduced(x, values_w, ss, away, here, True)
        values, inv = settle(kept, from_core, from_f, onehot)
        v2, v1 = along(values, 2), along(values, 1)
        a = attend(p, v2, v1, values, onehot)
        a_c = swap_c(a)
        a_f = swap_f(a)
        part = half(a, a_c, out_w, current, first)
        a_d = swap_c(a_f)
        records.append((current, inv, values))
        current, x, ss = update(a_f, a_d, out_w, part, second)
    final_state = assemble(*own_tokens(x, c), me[None].astype(jnp.int32), bf16)
    gradient = gb.astype(f32)
    zero = jnp.zeros((T, QF), f32)
    for cur, inv, values in reversed(records):
        kept, from_core, from_f = reduced(gb, out_w, ss, away, here, False)
        o2, o1, o0 = spread(kept, from_core, from_f, onehot, pt)
        r2, r1 = along(o2, -2), along(o1, -1)
        a = gather_grad(o0, r1, r2, values, onehot)
        a_c = swap_c(a)
        a_f = swap_f(a)
        part = half(a, a_c, values_w, zero, first)
        a_d = swap_c(a_f)
        gradient, gb = backstep(a_f, a_d, a, a_c, values_w, part, gradient, cur, inv, second)
    state_grad = assemble(*own_tokens(gb, c), me[None].astype(jnp.int32), f32)
    return (final_state, state_grad)


def solution(mesh):
    fine = Mesh(mesh.devices.reshape(2, 4, 4, 2, 2), ("yl", "x", "z", "c", "f"))
    seq = ("yl", "x", "z", "c")
    placed = (
        P(seq, None),
        P(seq, "f"),
        P(seq, "f"),
        P("f", seq, None),
        P("f", seq, None),
        P(),
        P(seq, None),
    )
    return jax.shard_map(
        local,
        mesh=fine,
        in_specs=placed,
        out_specs=(P(seq, None), P(seq, None)),
        check_vma=False,
    )
```

```python
import functools
import math

import jax
import jax.numpy as jnp
from jax import lax
from jax.experimental import pallas as pl
from jax.experimental.pallas import tpu as pltpu
from jax.sharding import Mesh
from jax.sharding import PartitionSpec as P

HEAD_DIM = 96
BLOCK = 128
REACH = 4
EPS = 1e-06

D = 5280
QF = 1320
T = 256
HQ = 672
HEADS_Q = 7
UNIT = 24
NPAD = 768
STAT = 192
CHIPS = 32

bf16 = jnp.bfloat16
f32 = jnp.float32
PARAMS = pltpu.CompilerParams(vmem_limit_bytes=56 * 1024 * 1024)
SWAP = [(0, 1), (1, 0)]


def dot(a, b):
    return jnp.dot(a, b, preferred_element_type=f32)


def dot_00(a, b):
    return lax.dot_general(a, b, (((0,), (0,)), ((), ())), preferred_element_type=f32)


def same(shape, count=2):
    zeros = (0,) * len(shape)
    return pl.BlockSpec(shape, lambda i, *s: zeros)


def split(row):
    hi = row.astype(bf16).astype(f32)
    return hi, row - hi


def spot_rows(spot, row):
    hi, lo = split(row)
    channel = lax.broadcasted_iota(jnp.int32, (STAT, 1), 0)
    at = UNIT * spot + 21
    return jnp.where(channel == at, hi, 0.0) + jnp.where(channel == at + 1, lo, 0.0)


def spot_sum(x, first):
    channel = lax.broadcasted_iota(jnp.int32, (STAT, 1), 0)
    group, inner = channel // UNIT, channel % UNIT
    mark = ((inner == 21) | (inner == 22)) & (group >= first) & (group < first + 4)
    return jnp.sum(jnp.where(mark, x[:STAT], 0.0), axis=0, keepdims=True)


WEIGHT = (16, 1, 1, 2 * UNIT, QF)


def weight_spec(which):
    return pl.BlockSpec(WEIGHT, lambda i, s: (0, which, s[i], 0, 0))


def project_body(sel, x_ref, g_ref, *rest, stats):
    o_ref = rest[-1]
    out = dot(g_ref[...].reshape(NPAD, QF), x_ref[...])
    o_ref[0] = out.astype(bf16)
    if stats:
        low = out[:STAT]
        for k in range(stats):
            low = low + spot_rows(4 * k + sel[2], rest[k][...])
        o_ref[0, :STAT] = low.astype(bf16)


def project(x, g, which, sel, rows):
    return pl.pallas_call(
        functools.partial(project_body, stats=len(rows)),
        out_shape=jax.ShapeDtypeStruct((2, NPAD, T), bf16),
        grid_spec=pltpu.PrefetchScalarGridSpec(
            num_scalar_prefetch=1,
            grid=(2,),
            in_specs=[same((QF, T)), weight_spec(which)] + [same((1, T))] * len(rows),
            out_specs=pl.BlockSpec((1, NPAD, T), lambda i, s: (i, 0, 0)),
        ),
        compiler_params=PARAMS,
        name="project",
    )(sel, x, g, *rows)


def settle_body(k_ref, c_ref, f_ref, pick_ref, v_ref, inv_ref, m_ref):
    v = k_ref[0].astype(f32) + c_ref[0].astype(f32) + f_ref[...].astype(f32)
    inv = lax.rsqrt(spot_sum(v, 0) * (1.0 / D) + EPS)
    v_ref[...] = dot(pick_ref[...], (v * inv).astype(bf16)).astype(bf16)
    inv_ref[...] = inv
    m_ref[...] = spot_sum(v, 4)


def settle(kept, from_core, from_f, pick):
    row = jax.ShapeDtypeStruct((1, T), f32)
    return pl.pallas_call(
        settle_body,
        out_shape=(jax.ShapeDtypeStruct((HQ, T), bf16), row, row),
        grid=(1,),
        in_specs=[same((1, NPAD, T)), same((1, NPAD, T)), same((NPAD, T)), same((HQ, NPAD))],
        out_specs=(same((HQ, T)), same((1, T)), same((1, T))),
        compiler_params=PARAMS,
        name="settle",
    )(kept, from_core, from_f, pick)


def softmax_body(q_ref, k2_ref, k1_ref, k0_ref, qd_ref, kd_ref, p_ref, pt_ref):
    key = lax.broadcasted_iota(jnp.int32, (3 * T, T), 0)
    query = lax.broadcasted_iota(jnp.int32, (3 * T, T), 1)
    ok = (qd_ref[...] == kd_ref[...]) & (key <= query + 2 * T)
    scale = 1.0 / math.sqrt(HEAD_DIM)
    for h in range(HEADS_Q):
        at = slice(HEAD_DIM * h, HEAD_DIM * (h + 1))
        q = q_ref[at]
        s = jnp.concatenate([dot_00(r[at], q) for r in (k2_ref, k1_ref, k0_ref)], axis=0)
        s = jnp.where(ok, s * scale, -1e30)
        top = jnp.max(s, axis=0, keepdims=True)
        e = jnp.where(ok, jnp.exp(s - top), 0.0)
        p = e / jnp.sum(e, axis=0, keepdims=True)
        pt_ref[h] = p.astype(bf16)
        p_ref[h] = p.T.astype(bf16)


def softmax(q, k2, k1, k0, qdoc, kdoc):
    return pl.pallas_call(
        softmax_body,
        out_shape=(
            jax.ShapeDtypeStruct((HEADS_Q, T, 3 * T), bf16),
            jax.ShapeDtypeStruct((HEADS_Q, 3 * T, T), bf16),
        ),
        compiler_params=PARAMS,
        name="softmax",
    )(q, k2, k1, k0, qdoc, kdoc)


def attend_body(pt_ref, v2_ref, v1_ref, v0_ref, pick_ref, o_ref, acc_ref):
    for h in range(HEADS_Q):
        at = slice(HEAD_DIM * h, HEAD_DIM * (h + 1))
        out = (
            dot(v2_ref[at], pt_ref[h, :T])
            + dot(v1_ref[at], pt_ref[h, T : 2 * T])
            + dot(v0_ref[at], pt_ref[h, 2 * T :])
        )
        acc_ref[at] = out.astype(bf16)
    o_ref[...] = dot_00(pick_ref[...], acc_ref[...]).astype(bf16)


def attend(pt, v2, v1, v0, pick):
    return pl.pallas_call(
        attend_body,
        out_shape=jax.ShapeDtypeStruct((NPAD, T), bf16),
        scratch_shapes=[pltpu.VMEM((HQ, T), bf16)],
        compiler_params=PARAMS,
        name="attend",
    )(pt, v2, v1, v0, pick)


def spread_body(k_ref, c_ref, f_ref, pick_ref, p_ref, o2_ref, o1_ref, o0_ref):
    v = k_ref[0].astype(f32) + c_ref[0].astype(f32) + f_ref[...].astype(f32)
    da = dot(pick_ref[...], v.astype(bf16)).astype(bf16)
    for h in range(HEADS_Q):
        at = slice(HEAD_DIM * h, HEAD_DIM * (h + 1))
        out = dot(da[at], p_ref[h]).astype(bf16)
        o2_ref[at] = out[:, :T]
        o1_ref[at] = out[:, T : 2 * T]
        o0_ref[at] = out[:, 2 * T :]


def spread(kept, from_core, from_f, pick, p):
    one = jax.ShapeDtypeStruct((HQ, T), bf16)
    return pl.pallas_call(
        spread_body,
        out_shape=(one, one, one),
        grid=(1,),
        in_specs=[
            same((1, NPAD, T)),
            same((1, NPAD, T)),
            same((NPAD, T)),
            same((HQ, NPAD)),
            same((HEADS_Q, T, 3 * T)),
        ],
        out_specs=(same((HQ, T)),) * 3,
        compiler_params=PARAMS,
        name="spread",
    )(kept, from_core, from_f, pick, p)


def collect_body(o_ref, r1_ref, r2_ref, v_ref, pick_ref, out_ref, *, stats):
    dv = o_ref[...].astype(f32) + r1_ref[...].astype(f32) + r2_ref[...].astype(f32)
    dv = dv.astype(bf16)
    out = dot_00(pick_ref[...], dv)
    out_ref[...] = out.astype(bf16)
    if stats:
        m = jnp.sum(dv.astype(f32) * v_ref[...].astype(f32), axis=0, keepdims=True)
        out_ref[:STAT] = (out[:STAT] + spot_rows(0, m)).astype(bf16)


def collect(own, r1, r2, values, pick, stats):
    return pl.pallas_call(
        functools.partial(collect_body, stats=stats),
        out_shape=jax.ShapeDtypeStruct((NPAD, T), bf16),
        compiler_params=PARAMS,
        name="collect",
    )(own, r1, r2, values, pick)


def half_body(sel, a_ref, b_ref, g_ref, *rest):
    o_ref = rest[-1]
    w = g_ref[...].reshape(NPAD, QF)

    @pl.when(pl.program_id(0) == 0)
    def _():
        out = dot_00(w, a_ref[...])
        o_ref[...] = out + rest[0][...] if len(rest) > 1 else out

    @pl.when(pl.program_id(0) == 1)
    def _():
        o_ref[...] += dot_00(w, b_ref[...])


def half(a, b, g, which, base, sel):
    more = () if base is None else (base,)
    return pl.pallas_call(
        half_body,
        out_shape=jax.ShapeDtypeStruct((QF, T), f32),
        grid_spec=pltpu.PrefetchScalarGridSpec(
            num_scalar_prefetch=1,
            grid=(2,),
            in_specs=[same((NPAD, T)), same((NPAD, T)), weight_spec(which)]
            + [same((QF, T))] * len(more),
            out_specs=same((QF, T)),
        ),
        compiler_params=PARAMS,
        name="half",
    )(sel, a, b, g, *more)


def update_body(sel, a_ref, b_ref, g_ref, part_ref, dn_ref, o_ref, x_ref, ss_ref, m_ref):
    w = g_ref[...].reshape(NPAD, QF)

    @pl.when(pl.program_id(0) == 0)
    def _():
        o_ref[...] = part_ref[...] + dot_00(w, a_ref[...])

    @pl.when(pl.program_id(0) == 1)
    def _():
        new = o_ref[...] + dot_00(w, b_ref[...])
        o_ref[...] = new
        x_ref[...] = new.astype(bf16)
        ss_ref[...] = jnp.sum(new * new, axis=0, keepdims=True)
        m_ref[...] = jnp.sum(new * dn_ref[...], axis=0, keepdims=True)


def update(a, b, g, which, part, dn, sel):
    row = jax.ShapeDtypeStruct((1, T), f32)
    return pl.pallas_call(
        update_body,
        out_shape=(
            jax.ShapeDtypeStruct((QF, T), f32),
            jax.ShapeDtypeStruct((QF, T), bf16),
            row,
            row,
        ),
        grid_spec=pltpu.PrefetchScalarGridSpec(
            num_scalar_prefetch=1,
            grid=(2,),
            in_specs=[same((NPAD, T)), same((NPAD, T)), weight_spec(which), same((QF, T)), same((QF, T))],
            out_specs=(same((QF, T)), same((QF, T)), same((1, T)), same((1, T))),
        ),
        compiler_params=PARAMS,
        name="update",
    )(sel, a, b, g, part, dn)


def halves_out(o_ref, new):
    new = new.astype(bf16)
    o_ref[0] = new[:, :BLOCK]
    o_ref[1] = new[:, BLOCK:]


def last_body(sel, a_ref, b_ref, g_ref, part_ref, o_ref, acc_ref):
    w = g_ref[...].reshape(NPAD, QF)

    @pl.when(pl.program_id(0) == 0)
    def _():
        acc_ref[...] = part_ref[...] + dot_00(w, a_ref[...])

    @pl.when(pl.program_id(0) == 1)
    def _():
        halves_out(o_ref, acc_ref[...] + dot_00(w, b_ref[...]))


def last(a, b, g, which, part, sel):
    return pl.pallas_call(
        last_body,
        out_shape=jax.ShapeDtypeStruct((2, QF, BLOCK), bf16),
        grid_spec=pltpu.PrefetchScalarGridSpec(
            num_scalar_prefetch=1,
            grid=(2,),
            in_specs=[same((NPAD, T)), same((NPAD, T)), weight_spec(which), same((QF, T))],
            out_specs=same((2, QF, BLOCK)),
            scratch_shapes=[pltpu.VMEM((QF, T), f32)],
        ),
        compiler_params=PARAMS,
        name="last",
    )(sel, a, b, g, part)


def backstep_body(sel, a_ref, b_ref, c_ref, d_ref, g_ref, part_ref, grad_ref, cur_ref, inv_ref, o_ref, acc_ref):
    w = g_ref[...].reshape(NPAD, QF)

    @pl.when(pl.program_id(0) == 0)
    def _():
        acc_ref[...] = part_ref[...] + dot_00(w, a_ref[...])

    @pl.when(pl.program_id(0) == 1)
    def _():
        d_normed = acc_ref[...] + dot_00(w, b_ref[...])
        m = jnp.zeros((1, T), f32)
        for r in (a_ref, b_ref, c_ref, d_ref):
            m = m + spot_sum(r[:STAT].astype(f32), 0)
        inv = inv_ref[...]
        halves_out(
            o_ref,
            grad_ref[...] + inv * (d_normed - cur_ref[...].astype(f32) * (inv * m * (1.0 / D))),
        )


def backstep(a, b, c, d, g, which, part, grad, current, inv, sel):
    act, wide = same((NPAD, T)), same((QF, T))
    return pl.pallas_call(
        backstep_body,
        out_shape=jax.ShapeDtypeStruct((2, QF, BLOCK), bf16),
        grid_spec=pltpu.PrefetchScalarGridSpec(
            num_scalar_prefetch=1,
            grid=(2,),
            in_specs=[act, act, act, act, weight_spec(which), wide, wide, wide, same((1, T))],
            out_specs=same((2, QF, BLOCK)),
            scratch_shapes=[pltpu.VMEM((QF, T), f32)],
        ),
        compiler_params=PARAMS,
        name="backstep",
    )(sel, a, b, c, d, g, part, grad, current, inv)


def assemble_body(sel, a_ref, b_ref, c_ref, d_ref, o_ref):
    for k, r in enumerate((a_ref, b_ref, c_ref, d_ref)):
        o_ref[sel[k]] = r[...].astype(o_ref.dtype)


def assemble(parts, sel, dtype):
    out = pl.pallas_call(
        assemble_body,
        out_shape=jax.ShapeDtypeStruct((4, QF, BLOCK), dtype),
        grid_spec=pltpu.PrefetchScalarGridSpec(
            num_scalar_prefetch=1,
            grid=(1,),
            in_specs=[same((QF, BLOCK))] * 4,
            out_specs=same((4, QF, BLOCK)),
        ),
        compiler_params=PARAMS,
        name="assemble",
    )(sel, *parts)
    return out.reshape(D, BLOCK).T


def swap_c(x):
    return lax.ppermute(x, "c", SWAP)


def swap_f(x):
    return lax.ppermute(x, "f", SWAP)


def along(x, steps):
    pairs = [(i, i + steps) for i in range(CHIPS) if 0 <= i + steps < CHIPS]
    return lax.ppermute(x, ("yl", "x", "z"), pairs)


def weight_quarter(wv, wo):
    rows = jnp.concatenate([wv, wo], 0)
    rows = jnp.pad(rows, ((0, 0), (0, UNIT - rows.shape[1]), (0, 0)))
    quarters = rows.reshape(2, UNIT, 2, 2, QF).transpose(2, 3, 0, 1, 4)
    sent = jnp.broadcast_to(quarters[:, None], (2, 2, 2, 2, UNIT, QF)).reshape(8, 2, UNIT, QF)
    got = lax.all_to_all(sent, ("f", "yl", "c"), 0, 0, tiled=True)
    return got.reshape(4, 2, 2, UNIT, QF).transpose(2, 0, 1, 3, 4).reshape(2, 4, 2 * UNIT, QF)


def token_quarter(x, f):
    part = lax.dynamic_slice_in_dim(x.T.reshape(2, 2, QF, BLOCK), f, 1, 0)[0]
    part = lax.all_to_all(part, "c", 0, 0, tiled=True)
    return part.transpose(1, 0, 2).reshape(QF, T)


def head_quarter(x):
    part = lax.all_to_all(x.T.reshape(2, HQ, BLOCK), "c", 0, 0, tiled=True)
    return part.transpose(1, 0, 2).reshape(HQ, T)


def own_tokens(x, c):
    mine = lax.dynamic_index_in_dim(x, c, 0, False)
    theirs = lax.dynamic_index_in_dim(x, 1 - c, 0, False)
    other = swap_c(theirs)
    return mine, other, swap_f(mine), swap_f(other)


def reduced(x, g, which, away, here, rows):
    sent = project(x, g, which, away, rows)
    from_core = swap_c(sent)
    kept = project(x, g, which, here, rows)
    from_f = swap_f(kept[1] + from_core[1])
    return kept, from_core, from_f


def local(state_in, query_vectors, key_vectors, value_weight, out_weight, doc_ids, cotangent):
    c = lax.axis_index("c")
    f = lax.axis_index("f")
    chip = (lax.axis_index("yl") * 4 + lax.axis_index("x")) * 4 + lax.axis_index("z")
    me = 2 * f + c
    near = 2 * f + (1 - c)
    far_c = 2 * (1 - f) + c
    far_d = 2 * (1 - f) + (1 - c)
    here = jnp.stack([me, far_c, me]).astype(jnp.int32)
    away = jnp.stack([near, far_d, me]).astype(jnp.int32)
    first = jnp.stack([me, near]).astype(jnp.int32)
    second = jnp.stack([far_c, far_d]).astype(jnp.int32)
    order = jnp.stack([me, near, far_c, far_d]).astype(jnp.int32)

    g = lax.all_gather(weight_quarter(value_weight, out_weight), ("x", "z"), axis=0)
    WV, WO = 0, 1

    pad_at = jnp.arange(NPAD)[None, :]
    nat_at = jnp.arange(HQ)[:, None]
    pick = ((pad_at // UNIT * 21 + pad_at % UNIT == nat_at) & (pad_at % UNIT < 21)).astype(bf16)

    docs = jnp.concatenate([jnp.full((REACH,), -1, jnp.int32), doc_ids])
    docs = lax.dynamic_slice_in_dim(docs, 2 * chip, REACH + 2, 0)
    kdoc = jnp.broadcast_to(docs[:, None], (REACH + 2, BLOCK)).reshape(3 * T, 1)
    qdoc = jnp.broadcast_to(docs[REACH:, None], (2, BLOCK)).reshape(1, T)
    q = head_quarter(query_vectors)
    k = head_quarter(key_vectors)
    p, pt = softmax(q, along(k, 2), along(k, 1), k, qdoc, kdoc)

    x0 = token_quarter(state_in, f)
    cot = token_quarter(cotangent, f)
    ss0 = jnp.sum(jnp.square(x0.astype(f32)), axis=0, keepdims=True)
    current0 = x0.astype(f32)
    x0, cot, ss0, current0, p, pt, pick = lax.optimization_barrier(
        (x0, cot, ss0, current0, p, pt, pick)
    )

    back = reduced(cot, g, WO, away, here, ())
    fore = reduced(x0, g, WV, away, here, (ss0,))
    values1, inv1, _ = settle(*fore, pick)
    v2, v1 = along(values1, 2), along(values1, 1)
    o2, o1, o0 = spread(*back, pick, p)
    r2, r1 = along(o2, -2), along(o1, -1)
    a = attend(pt, v2, v1, values1, pick)
    a_c, a_f = swap_c(a), swap_f(a)
    b = collect(o0, r1, r2, values1, pick, False)
    b_c, b_f = swap_c(b), swap_f(b)
    a_part = half(a, a_c, g, WO, current0, first)
    a_d = swap_c(a_f)
    b_part = half(b, b_c, g, WV, None, first)
    b_d = swap_c(b_f)
    dn2 = half(b_f, b_d, g, WV, b_part, second)
    current1, x1, ss1, raw = update(a_f, a_d, g, WO, a_part, dn2, second)

    fore = reduced(x1, g, WV, away, here, (ss1, raw))
    values2, inv2, m2 = settle(*fore, pick)
    grad1 = cot.astype(f32) + inv2 * (dn2 - current1 * (inv2 * inv2 * m2 * (1.0 / D)))
    back = reduced(grad1.astype(bf16), g, WO, away, here, ())
    v2, v1 = along(values2, 2), along(values2, 1)
    o2, o1, o0 = spread(*back, pick, p)
    r2, r1 = along(o2, -2), along(o1, -1)
    a = attend(pt, v2, v1, values2, pick)
    a_c, a_f = swap_c(a), swap_f(a)
    b = collect(o0, r1, r2, values1, pick, True)
    b_c, b_f = swap_c(b), swap_f(b)
    a_part = half(a, a_c, g, WO, current1, first)
    a_d = swap_c(a_f)
    b_part = half(b, b_c, g, WV, None, first)
    b_d = swap_c(b_f)
    final = last(a_f, a_d, g, WO, a_part, second)
    final_parts = own_tokens(final, c)
    grad0 = backstep(b_f, b_d, b, b_c, g, WV, b_part, grad1, x0, inv1, second)
    final_state = assemble(final_parts, order, bf16)
    state_grad = assemble(own_tokens(grad0, c), order, f32)
    return (final_state, state_grad)


def solution(mesh):
    fine = Mesh(mesh.devices.reshape(2, 4, 4, 2, 2), ("yl", "x", "z", "c", "f"))
    seq = ("yl", "x", "z", "c")
    placed = (
        P(seq, None),
        P(seq, "f"),
        P(seq, "f"),
        P("f", seq, None),
        P("f", seq, None),
        P(),
        P(seq, None),
    )
    return jax.shard_map(
        local,
        mesh=fine,
        in_specs=placed,
        out_specs=(P(seq, None), P(seq, None)),
        check_vma=False,
    )
```
